256 devices in a mesh: section: 4 (over z_lo, core), ctx: 64 (over y, x, z_hi).
Axes of the slice: x: 4, y: 4, z: 8 (z_hi: 4, z_lo: 2; z = z_hi * 2 + z_lo), core: 2. Of those that a mesh axis runs over, the one named last changes fastest.
Arguments:
- features: bfloat16 [4, 8192, 3, 1024], P('section', 'ctx'), may hold values from -6 to 6
- saved_conv: bfloat16 [4, 8192, 1024], P('section', 'ctx'), may hold values from -6 to 6
- grads_sent: bfloat16 [4, 8192, 1024], P('section', 'ctx'), may hold values from -6 to 6
- long_filter: float32 [4, 8192, 1024], P('section', 'ctx'), may hold values from -0.0625 to 0.0625
- short_taps: float32 [4, 3, 3, 1024], P('section'), may hold values from -3.5 to 3.5
Outputs:
- feature_grad: bfloat16 [4, 8192, 3, 1024], P('section', 'ctx')
- filter_grad: float32 [4, 8192, 1024], P('section', 'ctx')
The draws below stay inside these ranges and needn't reach their ends.
All inputs are finite; a program needn't handle non-finite values.
Results may differ from the reference program's by a relative error of at most 0.0049.
Values may be sent and summed in bfloat16 or wider, within the bound.
No kernel may reach another device: no remote copies, remote signals or barrier semaphores. Data moves between devices by JAX's collectives and lax.ppermute only.
A program may use at most 64 MiB of HBM per device.

```python
import jax
import jax.numpy as jnp
from jax import lax

CH = 1024
SECTIONS = 4
SEQ = 8192


def levels(stream_key, dims, cuts, least, largest):
    level = 1.0
    for position, parts in cuts:
        steps = jax.random.uniform(jax.random.fold_in(jax.random.fold_in(stream_key, 6), position), (parts,), jnp.float32, least / len(cuts), largest / len(cuts))
        level = level * jnp.repeat(jnp.exp(steps), dims[position] // parts).reshape((-1,) + (1,) * (len(dims) - 1 - position))
    return level


def scatter_about(key, dims, spread, most, cuts=(), kind=jnp.bfloat16):
    drawn = spread * jax.random.normal(key, dims, jnp.float32)
    if cuts:
        drawn = drawn * levels(key, dims, cuts, -0.22, 0.18)
    return jnp.clip(drawn, -most, most).astype(kind)


def setup_inputs(seed: int = 0) -> dict:
    seeds = jax.random.split(jax.random.key(seed), 6)
    features = scatter_about(seeds[0], (SECTIONS, SEQ, 3, CH), 1.0, 6.0, ((0, 4), (1, 64)))
    saved_conv = scatter_about(seeds[1], (SECTIONS, SEQ, CH), 1.0, 6.0, ((0, 4), (1, 64)))
    grads_sent = scatter_about(seeds[2], (SECTIONS, SEQ, CH), 1.0, 6.0, ((0, 4), (1, 64)))
    long_filter = scatter_about(seeds[3], (SECTIONS, SEQ, CH), SEQ ** -0.5, 0.0625, ((0, 4), (1, 64)), jnp.float32)
    short_taps = scatter_about(seeds[4], (SECTIONS, 3, 3, CH), 3 ** -0.5, 3.5, ((0, 4),), jnp.float32)
    return {"features": features, "saved_conv": saved_conv, "grads_sent": grads_sent, "long_filter": long_filter, "short_taps": short_taps}


def short_mix(signal, weights):
    length = signal.shape[0]
    padded = jnp.pad(signal, ((2, 0), (0, 0), (0, 0)))
    result = jnp.zeros_like(signal)
    for offset in range(3):
        result = result + weights[:, offset, :][None] * padded[2 - offset:2 - offset + length]
    return result


def adjoint_mix(upstream, weights):
    length = upstream.shape[0]
    padded = jnp.pad(upstream, ((0, 2), (0, 0), (0, 0)))
    result = jnp.zeros_like(upstream)
    for offset in range(3):
        result = result + weights[:, offset, :][None] * padded[offset:offset + length]
    return result


def one_section(operands):
    features, saved_conv, cotangent, long_filter, short_taps = operands
    length = features.shape[0]
    mixed = short_mix(features.astype(jnp.float32), short_taps)
    query = mixed[:, 0]
    key_branch = mixed[:, 1]
    value_branch = mixed[:, 2]
    upstream = cotangent.astype(jnp.float32)
    product = key_branch * value_branch
    pulled = query * upstream
    padded_length = 2 * length
    filter_spec = jnp.fft.fft(long_filter, n=padded_length, axis=0)
    product_spec = jnp.fft.fft(product, n=padded_length, axis=0)
    pulled_spec = jnp.fft.fft(pulled, n=padded_length, axis=0)
    conv_grad = jnp.real(jnp.fft.ifft(jnp.conj(filter_spec) * pulled_spec, axis=0))[:length]
    lag_grad = jnp.real(jnp.fft.ifft(jnp.conj(product_spec) * pulled_spec, axis=0))[:length]
    grad_query = (upstream * saved_conv.astype(jnp.float32)).astype(jnp.bfloat16)
    grad_key = (conv_grad * value_branch).astype(jnp.bfloat16)
    grad_value = (conv_grad * key_branch).astype(jnp.bfloat16)
    stacked = jnp.stack([grad_query, grad_key, grad_value], axis=1).astype(jnp.float32)
    feature_grad = adjoint_mix(stacked, short_taps).astype(jnp.bfloat16)
    return feature_grad, lag_grad * (SEQ ** -0.5)


def reference(features, saved_conv, grads_sent, long_filter, short_taps):
    incoming = jnp.roll(grads_sent, -1, axis=0)
    feature_grad, filter_grad = lax.map(one_section, (features, saved_conv, incoming, long_filter, short_taps))
    return feature_grad, filter_grad
```

```python
import functools
import math

import jax
import jax.numpy as jnp
import numpy as np
from jax import lax
from jax.experimental import pallas as pl
from jax.experimental.pallas import tpu as pltpu
from jax.sharding import PartitionSpec as P

F32 = jnp.float32
BF16 = jnp.bfloat16
VMEM = pl.BlockSpec(memory_space=pltpu.VMEM)
LANES = 128


def params():
    return pltpu.CompilerParams(vmem_limit_bytes=24 * 1024 * 1024)


def two_parts(table):
    high = table.astype(np.float32).astype(BF16)
    low = (table - high.astype(np.float64)).astype(np.float32).astype(BF16)
    return high, low


def tables(blocks, rows):
    length = blocks * rows
    k1 = np.arange(blocks)
    a = np.arange(blocks)
    b = np.arange(rows)
    outer = 2 * np.pi * np.outer(k1 + 0.25, a) / blocks
    phase = 2 * np.pi * np.outer(k1 + 0.25, b) / length
    inner = 2 * np.pi * (np.outer(b, b) % rows) / rows
    cos, sin = np.cos(inner), np.sin(inner)
    first = np.concatenate([np.cos(outer), -np.sin(outer)], axis=0)
    first_high, first_low = two_parts(first)
    first_table = np.concatenate([first_high, first_low], axis=1)
    second = np.block([[cos, -sin], [sin, cos]])
    back = np.block([[cos, sin], [-sin, cos]])
    last = np.concatenate([np.cos(outer).T, -np.sin(outer).T], axis=1) / length
    phases = np.stack([np.cos(phase), np.sin(phase)]).astype(np.float32)
    return (
        first_table,
        np.stack(two_parts(second)),
        np.stack(two_parts(back)),
        np.stack(two_parts(last)),
        phases,
    )


def dot(left, right):
    return jnp.dot(left, right, preferred_element_type=F32)


def split_value(value):
    high = value.astype(BF16)
    low = (value - high.astype(F32)).astype(BF16)
    return high, low


def mixed_branch(x_ref, before_ref, taps_ref, branch, lanes):
    now = x_ref[branch, :, lanes].astype(F32)
    before = before_ref[branch, :, lanes].astype(F32)
    count = now.shape[0]
    whole = jnp.concatenate([before, now], axis=0)
    edge = before.shape[0]
    total = taps_ref[branch, 0, :, lanes] * now
    for offset in (1, 2):
        total = total + taps_ref[branch, offset, :, lanes] * whole[edge - offset : edge - offset + count]
    return total


def before_kernel(x_ref, before_ref, taps_ref, incoming_ref, filter_ref, send_ref, key_ref, value_ref):
    peers = send_ref.shape[0]
    own = send_ref.shape[1] // 3
    width = x_ref.shape[2]
    per = LANES // own
    for group in range(width // LANES):
        lanes = slice(group * LANES, (group + 1) * LANES)
        query = mixed_branch(x_ref, before_ref, taps_ref, 0, lanes)
        key = mixed_branch(x_ref, before_ref, taps_ref, 1, lanes)
        value = mixed_branch(x_ref, before_ref, taps_ref, 2, lanes)
        key_ref[:, lanes] = key
        value_ref[:, lanes] = value
        pulled = query * incoming_ref[:, lanes].astype(F32)
        for member, signal in enumerate((filter_ref[:, lanes], key * value, pulled)):
            turned = signal.T.astype(BF16).reshape(per, own, signal.shape[0])
            send_ref[group * per : (group + 1) * per, member * own : (member + 1) * own, :] = turned


def channel_kernel(own, batch, got_ref, first_ref, second_ref, back_ref, last_ref, phase_ref, out_ref, wide, result):
    blocks = phase_ref.shape[1]
    rows = phase_ref.shape[2]
    wide[...] = got_ref[...].astype(F32)
    cos = phase_ref[0]
    sin = phase_ref[1]
    first = first_ref[...]
    second_high, second_low = second_ref[0], second_ref[1]
    back_high, back_low = back_ref[0], back_ref[1]
    last_high, last_low = last_ref[0], last_ref[1]
    for start in range(0, own, batch):
        signals = [
            wide[pl.ds(member * own + start + c, blocks, stride=3 * own), :].astype(BF16)
            for member in range(3)
            for c in range(batch)
        ]
        grid = jnp.concatenate(signals, axis=1)
        outer = dot(first, jnp.concatenate([grid, grid], axis=0))
        turned = []
        for index in range(3 * batch):
            real = outer[:blocks, index * rows : (index + 1) * rows]
            imag = outer[blocks:, index * rows : (index + 1) * rows]
            turned.append(jnp.concatenate([real * cos + imag * sin, imag * cos - real * sin], axis=1))
        high, low = split_value(jnp.concatenate(turned, axis=0))
        spec = dot(high, second_high) + (dot(low, second_high) + dot(high, second_low))
        size = batch * blocks
        filter_real, filter_imag = spec[:size, :rows], spec[:size, rows:]
        product_real, product_imag = spec[size : 2 * size, :rows], spec[size : 2 * size, rows:]
        pulled_real, pulled_imag = spec[2 * size :, :rows], spec[2 * size :, rows:]
        conv = jnp.concatenate(
            [
                filter_real * pulled_real + filter_imag * pulled_imag,
                filter_real * pulled_imag - filter_imag * pulled_real,
            ],
            axis=1,
        )
        lag = jnp.concatenate(
            [
                product_real * pulled_real + product_imag * pulled_imag,
                product_real * pulled_imag - product_imag * pulled_real,
            ],
            axis=1,
        )
        high, low = split_value(jnp.concatenate([conv, lag], axis=0))
        inner = dot(high, back_high) + (dot(low, back_high) + dot(high, back_low))
        columns = []
        for index in range(2 * batch):
            real = inner[index * blocks : (index + 1) * blocks, :rows]
            imag = inner[index * blocks : (index + 1) * blocks, rows:]
            columns.append(jnp.concatenate([real * cos - imag * sin, real * sin + imag * cos], axis=0))
        high, low = split_value(jnp.concatenate(columns, axis=1))
        signal = dot(last_high, high) + (dot(last_high, low) + dot(last_low, high))
        for member in range(2):
            for c in range(batch):
                index = member * batch + c
                result[pl.ds(member * own + start + c, blocks, stride=2 * own), :] = signal[
                    :, index * rows : (index + 1) * rows
                ]
    out_ref[...] = result[...].astype(BF16)


def gathered(got_ref, group, member):
    own = got_ref.shape[1] // 2
    per = LANES // own
    piece = got_ref[group * per : (group + 1) * per, member * own : (member + 1) * own, :]
    return piece.reshape(per * own, piece.shape[2]).astype(F32).T


def branch_kernel(got_ref, key_ref, value_ref, incoming_ref, saved_ref, out_ref):
    for group in range(key_ref.shape[1] // LANES):
        lanes = slice(group * LANES, (group + 1) * LANES)
        conv = gathered(got_ref, group, 0)
        query_grad = incoming_ref[:, lanes].astype(F32) * saved_ref[:, lanes].astype(F32)
        out_ref[0, :, lanes] = query_grad.astype(BF16)
        out_ref[1, :, lanes] = (conv * value_ref[:, lanes]).astype(BF16)
        out_ref[2, :, lanes] = (conv * key_ref[:, lanes]).astype(BF16)


def lag_kernel(scale, got_ref, out_ref):
    for group in range(out_ref.shape[1] // LANES):
        lanes = slice(group * LANES, (group + 1) * LANES)
        out_ref[:, lanes] = gathered(got_ref, group, 1) * scale


def after_kernel(grads_ref, after_ref, taps_ref, out_ref):
    count = grads_ref.shape[1]
    for group in range(grads_ref.shape[2] // LANES):
        lanes = slice(group * LANES, (group + 1) * LANES)
        for branch in range(3):
            now = grads_ref[branch, :, lanes].astype(F32)
            after = after_ref[branch, :, lanes].astype(F32)
            whole = jnp.concatenate([now, after], axis=0)
            total = taps_ref[branch, 0, :, lanes] * now
            for offset in (1, 2):
                total = total + taps_ref[branch, offset, :, lanes] * whole[offset : offset + count]
            out_ref[branch, :, lanes] = total.astype(BF16)


def shape(dims, kind):
    return jax.ShapeDtypeStruct(dims, kind)


def cost(flops, moved):
    return pl.CostEstimate(flops=flops, bytes_accessed=moved, transcendentals=0)


EDGE = 8


def shards(features, saved_conv, grads_sent, long_filter, short_taps):
    sections = lax.axis_size("section")
    devices = lax.axis_size("ctx")
    incoming = lax.ppermute(grads_sent[0], "section", [(i, (i - 1) % sections) for i in range(sections)])
    local = jnp.swapaxes(features[0], 0, 1)
    _, rows, width = local.shape
    own = width // devices
    taps = short_taps[0][:, :, None, :]
    before = lax.ppermute(local[:, rows - EDGE :], "ctx", [(i, i + 1) for i in range(devices - 1)])
    send, key, value = pl.pallas_call(
        before_kernel,
        out_shape=(
            shape((devices, 3 * own, rows), BF16),
            shape((rows, width), F32),
            shape((rows, width), F32),
        ),
        in_specs=[VMEM] * 5,
        out_specs=(VMEM,) * 3,
        compiler_params=params(),
        cost_estimate=cost(20 * rows * width, 12 * rows * width),
        name="before",
    )(local, before, taps, incoming, long_filter[0])
    got = lax.all_to_all(send, "ctx", split_axis=0, concat_axis=0, tiled=True)
    constants = tables(devices, rows)
    back = pl.pallas_call(
        functools.partial(channel_kernel, own, 4),
        out_shape=shape((devices * 2 * own, rows), BF16),
        in_specs=[VMEM] * 6,
        out_specs=VMEM,
        scratch_shapes=[
            pltpu.VMEM((devices * 3 * own, rows), F32),
            pltpu.VMEM((devices * 2 * own, rows), F32),
        ],
        compiler_params=params(),
        cost_estimate=cost(4000 * rows * width, 6 * rows * width),
        name="channels",
    )(got.reshape(devices * 3 * own, rows), *constants)
    returned = lax.all_to_all(
        back.reshape(devices, 2 * own, rows), "ctx", split_axis=0, concat_axis=0, tiled=True
    )
    grads = pl.pallas_call(
        branch_kernel,
        out_shape=shape((3, rows, width), BF16),
        in_specs=[VMEM] * 5,
        out_specs=VMEM,
        compiler_params=params(),
        cost_estimate=cost(6 * rows * width, 18 * rows * width),
        name="branches",
    )(returned, key, value, incoming, saved_conv[0])
    after = lax.ppermute(grads[:, :EDGE], "ctx", [(i + 1, i) for i in range(devices - 1)])
    filter_grad = pl.pallas_call(
        functools.partial(lag_kernel, (rows * devices) ** -0.5),
        out_shape=shape((rows, width), F32),
        in_specs=[VMEM],
        out_specs=VMEM,
        compiler_params=params(),
        cost_estimate=cost(2 * rows * width, 6 * rows * width),
        name="lags",
    )(returned)
    feature_grad = pl.pallas_call(
        after_kernel,
        out_shape=shape((3, rows, width), BF16),
        in_specs=[VMEM] * 3,
        out_specs=VMEM,
        compiler_params=params(),
        cost_estimate=cost(15 * rows * width, 12 * rows * width),
        name="after",
    )(grads, after, taps)
    return (jnp.swapaxes(feature_grad, 0, 1)[None], filter_grad[None])


def solution(mesh):
    placed = (
        P("section", "ctx", None, None),
        P("section", "ctx", None),
        P("section", "ctx", None),
        P("section", "ctx", None),
        P("section", None, None, None),
    )
    return jax.shard_map(
        shards,
        mesh=mesh,
        in_specs=placed,
        out_specs=(P("section", "ctx", None, None), P("section", "ctx", None)),
        check_vma=False,
    )
```

```python
import functools

import jax
import jax.numpy as jnp
import numpy as np
from jax import lax
from jax.experimental import pallas as pl
from jax.experimental.pallas import tpu as pltpu
from jax.sharding import PartitionSpec as P


F32 = jnp.float32
BF16 = jnp.bfloat16
VMEM = pl.BlockSpec(memory_space=pltpu.VMEM)
LANES = 128
EDGE = 8
COLUMNS = 256


def params(size=24 * 1024):
    return pltpu.CompilerParams(vmem_limit_bytes=size * 1024)


def two_parts(table):
    high = table.astype(np.float32).astype(BF16)
    low = (table - high.astype(np.float64)).astype(np.float32).astype(BF16)
    return high, low


def stacked_parts(table, axis, order):
    parts = two_parts(table)
    return np.concatenate([parts[index] for index in order], axis=axis)


def tables(blocks, rows):
    length = blocks * rows
    k1 = np.arange(blocks)
    a = np.arange(blocks)
    b = np.arange(rows)
    outer = 2 * np.pi * np.outer(k1 + 0.25, a) / blocks
    phase = 2 * np.pi * np.outer(k1 + 0.25, b) / length
    inner = 2 * np.pi * (np.outer(b, b) % rows) / rows
    cos, sin = np.cos(inner), np.sin(inner)
    first = np.concatenate([np.cos(outer), -np.sin(outer)], axis=0)
    first_high, first_low = two_parts(first)
    first_table = np.concatenate([first_high, first_low], axis=1)
    second = np.block([[cos, -sin], [sin, cos]])
    back = np.block([[cos, sin], [-sin, cos]])
    last = np.concatenate([np.cos(outer).T, -np.sin(outer).T], axis=1) / length
    following = np.concatenate([last[1:], np.zeros_like(last[:1])], axis=0)
    phases = np.stack([np.cos(phase), np.sin(phase)]).astype(np.float32)
    return (
        first_table,
        stacked_parts(second, 0, (0, 1)),
        stacked_parts(back, 0, (0, 1)),
        np.stack([stacked_parts(each, 1, (0, 0, 1)) for each in (last, following)]),
        phases,
    )


def dot(left, right):
    return jnp.dot(left, right, preferred_element_type=F32)


def split_value(value):
    high = value.astype(BF16)
    low = (value - high.astype(F32)).astype(BF16)
    return high, low


def mixed_branch(x_ref, before_ref, taps_ref, branch, lanes):
    now = x_ref[branch, :, lanes].astype(F32)
    before = before_ref[branch, :, lanes].astype(F32)
    count = now.shape[0]
    whole = jnp.concatenate([before, now], axis=0)
    edge = before.shape[0]
    total = taps_ref[branch, 0, :, lanes] * now
    for offset in (1, 2):
        total = total + taps_ref[branch, offset, :, lanes] * whole[edge - offset : edge - offset + count]
    return total


def turned(signal, own):
    return signal.T.astype(BF16).reshape(LANES // own, own, signal.shape[0])


def fetch_kernel(x_hbm, x_ref, sem):
    copy = pltpu.make_async_copy(x_hbm, x_ref, sem)
    copy.start()
    copy.wait()


def before_kernel(
    x_ref, before_ref, taps_ref, filter_ref, incoming_ref, send_ref, key_ref, value_ref
):
    own = send_ref.shape[1] // 3
    per = LANES // own
    for group in range(x_ref.shape[2] // LANES):
        lanes = slice(group * LANES, (group + 1) * LANES)
        peers = slice(group * per, (group + 1) * per)
        query = mixed_branch(x_ref, before_ref, taps_ref, 0, lanes)
        key = mixed_branch(x_ref, before_ref, taps_ref, 1, lanes)
        value = mixed_branch(x_ref, before_ref, taps_ref, 2, lanes)
        key_ref[:, lanes] = key
        value_ref[:, lanes] = value
        upstream = incoming_ref[:, lanes].astype(F32)
        for member, signal in enumerate((filter_ref[:, lanes], key * value, query * upstream)):
            send_ref[peers, member * own : (member + 1) * own, :] = turned(signal, own)


def channel_kernel(
    own, batch, got_ref, first_ref, second_ref, back_ref, last_ref, phase_ref, out_ref, wide, result, edges
):
    blocks = phase_ref.shape[1]
    rows = phase_ref.shape[2]
    wide[...] = got_ref[...].astype(F32)
    cos = phase_ref[0]
    sin = phase_ref[1]
    first = first_ref[...]
    second = second_ref[...]
    back = back_ref[...]
    lane = lax.broadcasted_iota(jnp.int32, (2 * blocks, LANES), 1) - own * lax.rem(lax.axis_index("ctx"), LANES // own)
    ahead = [jnp.zeros((2 * blocks, LANES), F32)] * 2
    for start in range(0, own, batch):
        signals = [
            wide[pl.ds(member * own + start + c, blocks, stride=3 * own), :].astype(BF16)
            for member in range(3)
            for c in range(batch)
        ]
        grid = jnp.concatenate(signals, axis=1)
        outer = dot(first, jnp.concatenate([grid, grid], axis=0))
        pieces = []
        for index in range(3 * batch):
            real = outer[:blocks, index * rows : (index + 1) * rows]
            imag = outer[blocks:, index * rows : (index + 1) * rows]
            pieces.append(jnp.concatenate([real * cos + imag * sin, imag * cos - real * sin], axis=1))
        high = jnp.concatenate(pieces, axis=0).astype(BF16)
        spec = dot(jnp.concatenate([high, high], axis=1), second)
        size = batch * blocks
        filter_real, filter_imag = spec[:size, :rows], spec[:size, rows:]
        product_real, product_imag = spec[size : 2 * size, :rows], spec[size : 2 * size, rows:]
        pulled_real, pulled_imag = spec[2 * size :, :rows], spec[2 * size :, rows:]
        conv = jnp.concatenate(
            [
                filter_real * pulled_real + filter_imag * pulled_imag,
                filter_real * pulled_imag - filter_imag * pulled_real,
            ],
            axis=1,
        )
        lag = jnp.concatenate(
            [
                product_real * pulled_real + product_imag * pulled_imag,
                product_real * pulled_imag - product_imag * pulled_real,
            ],
            axis=1,
        )
        high = jnp.concatenate([conv, lag], axis=0).astype(BF16)
        inner = dot(jnp.concatenate([high, high], axis=1), back)
        columns = []
        for index in range(2 * batch):
            real = inner[index * blocks : (index + 1) * blocks, :rows]
            imag = inner[index * blocks : (index + 1) * blocks, rows:]
            columns.append(jnp.concatenate([real * cos - imag * sin, real * sin + imag * cos], axis=0))
        for c in range(batch):
            for j in range(2):
                ahead[j] = jnp.where(lane == start + c, columns[c][:, j : j + 1], ahead[j])
        high, low = split_value(jnp.concatenate(columns, axis=1))
        signal = dot(last_ref[0], jnp.concatenate([high, low, high], axis=0))
        for member in range(2):
            for c in range(batch):
                index = member * batch + c
                result[pl.ds(member * own + start + c, blocks, stride=2 * own), :] = signal[
                    :, index * rows : (index + 1) * rows
                ]
    out_ref[:, :own] = result[...].astype(BF16).reshape(blocks, own, 2, rows)
    high, low = split_value(jnp.concatenate(ahead, axis=1))
    further = dot(last_ref[1], jnp.concatenate([high, low, high], axis=0))
    for j in range(2):
        edges[pl.ds(j, blocks, stride=2), :] = further[:, j * LANES : (j + 1) * LANES]
    out_ref[:, own] = edges[...].astype(BF16).reshape(blocks, 2, LANES)


def after_kernel(
    scale, got_ref, key_ref, value_ref, incoming_ref, saved_ref, edge_ref, taps_ref, out_ref, filter_ref
):
    own = got_ref.shape[1] - 1
    per = LANES // own
    rows, width = key_ref.shape
    for group in range(width // LANES):
        lanes = slice(group * LANES, (group + 1) * LANES)
        peers = slice(group * per, (group + 1) * per)
        conv = got_ref[peers, : own // 2].reshape(LANES, rows).astype(F32).T
        lag = got_ref[peers, own // 2 : own].reshape(LANES, rows).astype(F32).T
        filter_ref[:, lanes] = lag * scale
        further = jnp.sum(got_ref[peers, own].astype(F32), axis=0)
        further = jnp.concatenate([further, jnp.zeros((EDGE - 2, LANES), F32)], axis=0)
        grads = (
            incoming_ref[:, lanes].astype(F32) * saved_ref[:, lanes].astype(F32),
            conv * value_ref[:, lanes],
            conv * key_ref[:, lanes],
        )
        after = (
            edge_ref[0, :, lanes],
            further * edge_ref[2, :, lanes],
            further * edge_ref[1, :, lanes],
        )
        for branch in range(3):
            whole = jnp.concatenate([grads[branch], after[branch]], axis=0).astype(BF16).astype(F32)
            total = taps_ref[branch, 0, :, lanes] * whole[:rows]
            for offset in (1, 2):
                total = total + taps_ref[branch, offset, :, lanes] * whole[offset : offset + rows]
            out_ref[branch, :, lanes] = total.astype(BF16)


def shape(dims, kind):
    return jax.ShapeDtypeStruct(dims, kind)


def cost(flops, moved):
    return pl.CostEstimate(flops=flops, bytes_accessed=moved, transcendentals=0)


def section_part(features, saved_conv, grads_sent, long_filter, short_taps):
    sections = lax.axis_size("section")
    devices = lax.axis_size("ctx")
    incoming = lax.ppermute(grads_sent[0], "section", [(i, (i - 1) % sections) for i in range(sections)])
    local = jnp.swapaxes(features[0], 0, 1)
    _, rows, width = local.shape
    own = width // devices
    taps = short_taps[0][:, :, None, :]
    before = lax.ppermute(local[:, rows - EDGE :], "ctx", [(i, i + 1) for i in range(devices - 1)])
    outside = pl.BlockSpec(memory_space=pltpu.HBM)
    held = pl.pallas_call(
        fetch_kernel,
        out_shape=shape((3, rows, width), BF16),
        in_specs=[outside],
        out_specs=VMEM,
        scratch_shapes=[pltpu.SemaphoreType.DMA],
        compiler_params=params(54100),
        cost_estimate=cost(0, 20 * rows * width),
        name="fetch",
    )(local)
    send, key, value = pl.pallas_call(
        before_kernel,
        out_shape=(
            shape((devices, 3 * own, rows), BF16),
            shape((rows, width), F32),
            shape((rows, width), F32),
        ),
        in_specs=[VMEM] * 5,
        out_specs=(VMEM,) * 3,
        compiler_params=params(),
        cost_estimate=cost(20 * rows * width, 12 * rows * width),
        name="before",
    )(held, before, taps, long_filter[0], incoming)
    got = lax.all_to_all(send, "ctx", split_axis=0, concat_axis=0, tiled=True)
    query_edge = incoming[:EDGE].astype(F32) * saved_conv[0, :EDGE].astype(F32)
    edge = jnp.stack([query_edge, key[:EDGE], value[:EDGE]])
    edge = lax.ppermute(edge, "ctx", [(i + 1, i) for i in range(devices - 1)])
    back = pl.pallas_call(
        functools.partial(channel_kernel, own, 8),
        out_shape=shape((devices, own + 1, 2, rows), BF16),
        in_specs=[VMEM] * 6,
        out_specs=VMEM,
        scratch_shapes=[
            pltpu.VMEM((devices * 3 * own, rows), F32),
            pltpu.VMEM((devices * 2 * own, rows), F32),
            pltpu.VMEM((devices * 2, LANES), F32),
        ],
        compiler_params=params(),
        cost_estimate=cost(4000 * rows * width, 6 * rows * width),
        name="channels",
    )(got.reshape(devices * 3 * own, rows), *tables(devices, rows))
    returned = lax.all_to_all(back, "ctx", split_axis=0, concat_axis=0, tiled=True)
    steps = width // COLUMNS
    wide_block = pl.BlockSpec((rows, COLUMNS), lambda i: (0, i))
    deep_block = pl.BlockSpec((3, rows, COLUMNS), lambda i: (0, 0, i))
    feature_grad, filter_grad = pl.pallas_call(
        functools.partial(after_kernel, (rows * devices) ** -0.5),
        grid=(steps,),
        out_shape=(shape((3, rows, width), BF16), shape((rows, width), F32)),
        in_specs=[
            pl.BlockSpec((devices // steps, own + 1, 2, rows), lambda i: (i, 0, 0, 0)),
            wide_block,
            wide_block,
            wide_block,
            wide_block,
            pl.BlockSpec((3, EDGE, COLUMNS), lambda i: (0, 0, i)),
            pl.BlockSpec((3, 3, 1, COLUMNS), lambda i: (0, 0, 0, i)),
        ],
        out_specs=(deep_block, wide_block),
        compiler_params=params(),
        cost_estimate=cost(25 * rows * width, 22 * rows * width),
        name="after",
    )(returned, key, value, incoming, saved_conv[0], edge, taps)
    return (jnp.swapaxes(feature_grad, 0, 1)[None], filter_grad[None])


def solution(mesh):
    placed = (
        P("section", "ctx", None, None),
        P("section", "ctx", None),
        P("section", "ctx", None),
        P("section", "ctx", None),
        P("section", None, None, None),
    )
    return jax.shard_map(
        section_part,
        mesh=mesh,
        in_specs=placed,
        out_specs=(P("section", "ctx", None, None), P("section", "ctx", None)),
        check_vma=False,
    )
```
